512 devices in a mesh: section: 8 (over y), ident: 64 (over z, x, core).
Axes of the slice: x: 4, y: 8, z: 8, core: 2. Of those that a mesh axis runs over, the one named last changes fastest.
Arguments:
- inputs: bfloat16 [64, 192, 1024], P('ident'), may hold values from -6 to 6
- section_weight: bfloat16 [8, 1024, 1024], P('section'), may hold values from -0.1875 to 0.1875
- section_gain: float32 [8, 1024], P('section'), may hold values from 0.25 to 1.75
- neck_weight: bfloat16 [1024, 512], replicated, may hold values from -0.1875 to 0.1875
- centers: bfloat16 [64, 2, 3, 128, 512], P('ident'), may hold values from -6 to 6
- sampled: int32 [64, 2], P('ident'), may hold values from 0 to 255, as said below
- labels: int32 [64, 192], P('ident', 'section'), may hold values from 0 to 2097151, as said below
Outputs:
- embed_grad: float32 [64, 192, 512], P('ident', 'section')
The draws below stay inside these ranges and needn't reach their ends.
Inputs may be any that keep to these rules, and one draw needn't show every extreme that they name: `sampled`: the 2 block numbers of one shard are distinct. `labels`: every label is i * 256 * 128 + sampled[i, a] 128 + t for some shard i, slot a and position t.
All inputs are finite; a program needn't handle non-finite values.
Results may differ from the reference program's by a relative error of at most 0.008.
Values may be sent and summed in bfloat16 or wider, within the bound.
No kernel may reach another device: no remote copies, remote signals or barrier semaphores. Data moves between devices by JAX's collectives and lax.ppermute only.
A program may use at most 64 MiB of HBM per device.

```python
import math
import jax
import jax.numpy as jnp
from jax import lax

D = 1024
E = 512
SUB = 3
BLK = 128
BLOCKS_DEV = 256
SAMP_DEV = 2
ROWS = 192
N_SECTION = 8
N_IDENT = 64


def pick_blocks(key):
    shard_keys = jax.random.split(jax.random.fold_in(key, 11), N_IDENT)

    def order_one(shard_key):
        return jax.random.permutation(shard_key, BLOCKS_DEV)
    orders = jax.vmap(order_one)(shard_keys)
    return orders[:, :SAMP_DEV].astype(jnp.int32)


def draw_sampled(key, part):
    return pick_blocks(key)


def draw_labels(key, part):
    chosen = pick_blocks(key)
    owner = jax.random.randint(jax.random.fold_in(key, 21), (N_IDENT, ROWS), 0, N_IDENT)
    slot_pick = jax.random.randint(jax.random.fold_in(key, 22), (N_IDENT, ROWS), 0, SAMP_DEV)
    offset = jax.random.randint(jax.random.fold_in(key, 23), (N_IDENT, ROWS), 0, BLK)
    block_pick = chosen[owner, slot_pick]
    return (owner * (BLOCKS_DEV * BLK) + block_pick * BLK + offset).astype(jnp.int32)


def steps_of(own_key, dims, pieces, least, high):
    factor_of, own = 1.0, jax.random.fold_in(own_key, 6)
    for position, blocks in pieces:
        draws = jnp.exp(jax.random.uniform(jax.random.fold_in(own, position), (blocks,), jnp.float32, least / len(pieces), high / len(pieces)))
        factor_of = factor_of * jnp.repeat(draws, dims[position] // blocks).reshape([-1 if axis == position else 1 for axis in range(len(dims))])
    return factor_of


def bell_draw(key, dims, deviation, reach, pieces=(), held_as=jnp.bfloat16):
    drawn = deviation * jax.random.normal(key, dims, jnp.float32)
    if pieces:
        drawn = drawn * steps_of(key, dims, pieces, -0.22, 0.18)
    return jnp.clip(drawn, -reach, reach).astype(held_as)


def setup_inputs(seed: int = 0) -> dict:
    arg_keys = jax.random.split(jax.random.key(seed), 8)
    inputs = bell_draw(arg_keys[0], (N_IDENT, ROWS, D), 1.0, 6.0, ((0, 64),))
    section_weight = bell_draw(arg_keys[1], (N_SECTION, D, D), D ** -0.5, 0.1875, ((0, 8),))
    section_gain = jnp.clip(1.0 + 0.15 * jax.random.normal(arg_keys[2], (N_SECTION, D), jnp.float32), 0.25, 1.75)
    neck_weight = bell_draw(arg_keys[3], (D, E), D ** -0.5, 0.1875)
    centers = bell_draw(arg_keys[4], (N_IDENT, SAMP_DEV, SUB, BLK, E), 1.0, 6.0, ((0, 64),))
    sampled = draw_sampled(jax.random.fold_in(arg_keys[7], 71), 0)
    labels = draw_labels(jax.random.fold_in(arg_keys[7], 71), 0)
    return {"inputs": inputs, "section_weight": section_weight, "section_gain": section_gain, "neck_weight": neck_weight, "centers": centers, "sampled": sampled, "labels": labels}


logit_scale = 64.0
pool_temp = 0.1
margin_angle = 0.5
sine_offset = 1.05

def layer_norm(values, gain):
    valf = values.astype(jnp.float32)
    center = valf - lax.optimization_barrier(jnp.mean(valf, axis=-1, keepdims=True))
    spread = lax.optimization_barrier(jnp.mean(center * center, axis=-1, keepdims=True))
    return center * lax.rsqrt(spread + 1e-06) * gain

def section_apply(trunk, weight, gain):
    normed = layer_norm(trunk, gain).astype(jnp.bfloat16)
    mixed = jnp.dot(normed, weight, preferred_element_type=jnp.float32)
    return (trunk.astype(jnp.float32) + jax.nn.gelu(mixed, approximate=False)).astype(jnp.bfloat16)

def unit_rows(values):
    valf = values.astype(jnp.float32)
    inverse = lax.rsqrt(lax.optimization_barrier(jnp.sum(valf * valf, axis=-1, keepdims=True)) + 1e-06)
    return (valf * inverse, inverse)

def shard_scores(feature, label_flat, unit_centers, picks, shard, nsamp, nsub, nblk):
    cosine = jnp.dot(feature, unit_centers.T, preferred_element_type=jnp.float32)
    cosine = cosine.reshape(feature.shape[0], nsamp, nsub, nblk)
    expo = jnp.exp(cosine / pool_temp)
    summed = lax.optimization_barrier(jnp.sum(expo, axis=2))
    pooled = pool_temp * jnp.log(summed / nsub)
    weights = expo / summed[:, :, None, :]
    idents = shard * (BLOCKS_DEV * nblk) + picks[:, None] * nblk + jnp.arange(nblk, dtype=jnp.int32)[None, :]
    target = label_flat[:, None, None] == idents[None, :, :]
    root_term = jnp.sqrt(sine_offset - pooled * pooled)
    margin = pooled * math.cos(margin_angle) - root_term * math.sin(margin_angle)
    logits = logit_scale * jnp.where(target, margin, pooled)
    slope = jnp.where(target, math.cos(margin_angle) + pooled * math.sin(margin_angle) / root_term, 1.0)
    return (logits, weights, target, slope)

def reference(inputs, section_weight, section_gain, neck_weight, centers, sampled, labels):
    nsamp = centers.shape[1]
    nsub = centers.shape[2]
    nblk = centers.shape[3]
    width = centers.shape[4]
    trunk = inputs.reshape(-1, inputs.shape[-1])
    for section in range(N_SECTION):
        trunk = section_apply(trunk, section_weight[section], section_gain[section])
    neck_in = layer_norm(trunk, 1.0).astype(jnp.bfloat16)
    embed = jnp.dot(neck_in, neck_weight, preferred_element_type=jnp.float32).astype(jnp.bfloat16)
    direction, inverse = unit_rows(embed)
    unit_embed = direction.astype(jnp.bfloat16)
    label_flat = labels.reshape(-1)
    shard_ids = jnp.arange(centers.shape[0], dtype=jnp.int32)

    def prepare(block):
        return unit_rows(block.reshape(-1, width))[0].astype(jnp.bfloat16)

    def total_step(carry, items):
        block, picks, shard = items
        logits = shard_scores(unit_embed, label_flat, prepare(block), picks, shard, nsamp, nsub, nblk)[0]
        return (carry + lax.optimization_barrier(jnp.sum(jnp.exp(logits), axis=(1, 2))), None)
    totals, _ = lax.scan(total_step, jnp.zeros((unit_embed.shape[0],), jnp.float32), (centers, sampled, shard_ids))

    def grad_step(carry, items):
        block, picks, shard = items
        unit_centers = prepare(block)
        logits, weights, target, slope = shard_scores(unit_embed, label_flat, unit_centers, picks, shard, nsamp, nsub, nblk)
        prob = jnp.exp(logits) / totals[:, None, None]
        factor = logit_scale * (prob - target.astype(jnp.float32)) * slope
        pulled = (factor[:, :, None, :] * weights).astype(jnp.bfloat16).reshape(unit_embed.shape[0], -1)
        return (carry + jnp.dot(pulled, unit_centers, preferred_element_type=jnp.float32), None)
    unit_grad, _ = lax.scan(grad_step, jnp.zeros((unit_embed.shape[0], width), jnp.float32), (centers, sampled, shard_ids))
    along = lax.optimization_barrier(jnp.sum(unit_grad * direction, axis=-1, keepdims=True))
    embed_grad = inverse * (unit_grad - along * direction)
    return embed_grad.reshape(inputs.shape[0], inputs.shape[1], width)
```

```python
import functools
import math

import jax
import jax.numpy as jnp
from jax import lax
from jax.experimental import pallas as pl
from jax.experimental.pallas import tpu as pltpu
from jax.sharding import PartitionSpec as P


BLOCKS_DEV = 256
Z, X, CORE = 8, 4, 2
PIECES = 4
DELAY = 2

logit_scale = 64.0
pool_temp = 0.1
margin_angle = 0.5
sine_offset = 1.05
f32, bf16 = jnp.float32, jnp.bfloat16
VMEM = pl.BlockSpec(memory_space=pltpu.VMEM)
SMEM = pl.BlockSpec(memory_space=pltpu.SMEM)


def ident_of(z, x, core):
    return (z % Z * X + x % X) * CORE + core


def ident_route(dx=0, flip=0):
    return [
        (ident_of(z, x, c), ident_of(z, x + dx, c ^ flip))
        for z in range(Z)
        for x in range(X)
        for c in range(CORE)
    ]


Z_GROUPS = [[ident_of(z, x, c) for z in range(Z)] for x in range(X) for c in range(CORE)]


def normed_of(values, gain):
    center = values - jnp.mean(values, axis=-1, keepdims=True)
    spread = jnp.mean(center * center, axis=-1, keepdims=True)
    normed = center * lax.rsqrt(spread + 1e-06)
    return normed if gain is None else normed * gain


def section_kernel(has_fresh, has_arrived, *refs):
    refs = list(refs)
    first = refs.pop(0)[0] if has_fresh and has_arrived else None
    fresh = refs.pop(0)[...].astype(f32) if has_fresh else None
    arrived = refs.pop(0)[...].astype(f32) if has_arrived else None
    weight, gain, out = refs
    if first is None:
        trunk = fresh if has_fresh else arrived
    else:
        trunk = jnp.where(first == 1, fresh, arrived)
    normed = normed_of(trunk, gain[...]).astype(bf16)
    mixed = jnp.dot(normed, weight[...], preferred_element_type=f32)
    half = 0.5 * mixed
    out[...] = (trunk + (half + half * lax.erf(mixed * math.sqrt(0.5)))).astype(bf16)


def section_call(first, fresh, arrived, weight, gain):
    has_fresh, has_arrived = fresh is not None, arrived is not None
    args, specs = [], []
    if has_fresh and has_arrived:
        args, specs = [first], [SMEM]
    rows = [a for a in (fresh, arrived) if a is not None]
    args += rows + [weight, gain]
    specs += [VMEM] * (len(rows) + 2)
    shape = rows[0].shape
    return pl.pallas_call(
        functools.partial(section_kernel, has_fresh, has_arrived),
        out_shape=jax.ShapeDtypeStruct(shape, bf16),
        in_specs=specs,
        out_specs=VMEM,
        name="section",
        cost_estimate=pl.CostEstimate(
            flops=2 * shape[0] * weight.shape[0] * weight.shape[1],
            bytes_accessed=2 * shape[0] * shape[1] * 2,
            transcendentals=shape[0] * shape[1],
        ),
    )(*args)


def neck_kernel(rows, weight, digits, sent, direction, inverse):
    width = weight.shape[1]
    neck_in = normed_of(rows[...].astype(f32), None).astype(bf16)
    embed = jnp.dot(neck_in, weight[...], preferred_element_type=f32).astype(bf16).astype(f32)
    inv = lax.rsqrt(jnp.sum(embed * embed, axis=-1, keepdims=True) + 1e-06)
    unit = embed * inv
    direction[...] = unit
    inverse[...] = jnp.broadcast_to(inv, inverse.shape)
    row = jnp.concatenate([unit.astype(bf16), digits[...]], axis=-1)
    for z in range(Z):
        sent[z] = row


def neck_call(rows, weight, digits):
    count, width = rows.shape[0], weight.shape[1]
    return pl.pallas_call(
        neck_kernel,
        out_shape=(
            jax.ShapeDtypeStruct((Z, count, width + 128), bf16),
            jax.ShapeDtypeStruct((count, width), f32),
            jax.ShapeDtypeStruct((count, 128), f32),
        ),
        in_specs=[VMEM] * 3,
        out_specs=(VMEM,) * 3,
        name="neck",
    )(rows, weight, digits)


def lane_of(block, lane):
    lanes = lax.broadcasted_iota(jnp.int32, block.shape, 1)
    return jnp.sum(jnp.where(lanes == lane, block, 0.0), axis=-1, keepdims=True)


def head_kernel(nsamp, nsub, nblk, feature, *refs):
    centers, (sent, grad, pull) = refs[:-3], refs[-3:]
    width = centers[0].shape[1]
    rows = feature.shape[0]
    unit = feature[:, :width]
    digits = feature[:, width:].astype(f32)
    label = (
        lane_of(digits, 0) * float(BLOCKS_DEV * nblk) + lane_of(digits, 1) * float(nblk) + lane_of(digits, 2)
    )
    step = lax.broadcasted_iota(jnp.int32, (1, nblk), 1).astype(f32)
    rest = jnp.zeros((rows, nblk), f32)
    pooled_target = jnp.zeros((rows, nblk), f32)
    hits = jnp.zeros((rows, nblk), f32)
    for turn, block in enumerate(centers):
        cosine = lax.dot_general(
            unit, block[: nsamp * nsub * nblk, :], (((1,), (1,)), ((), ())), preferred_element_type=f32
        )
        tail = block[nsamp * nsub * nblk :, :nblk].astype(f32)
        spread, chosen = [], []
        for a in range(nsamp):
            base = tail[0:1] * float(BLOCKS_DEV * nblk) + tail[a + 1 : a + 2] * float(nblk) + step
            target = label == base
            expo = []
            for k in range(nsub):
                at = (a * nsub + k) * nblk
                expo.append(jnp.exp(cosine[:, at : at + nblk] * (1.0 / pool_temp)))
            summed = functools.reduce(lambda p, q: p + q, expo)
            pooled = pool_temp * jnp.log(summed * (1.0 / nsub))
            each = jnp.where(target, 0.0, jnp.exp(logit_scale * pooled))
            share = 1.0 / summed
            rest += each
            hits += jnp.where(target, 1.0, 0.0)
            pooled_target += jnp.where(target, pooled, 0.0)
            scaled = each * share
            picked = jnp.where(target, share, 0.0)
            spread += [(e * scaled).astype(bf16) for e in expo]
            chosen += [(e * picked).astype(bf16) for e in expo]
        both = block[: nsamp * nsub * nblk, :]
        more = jnp.dot(jnp.concatenate(spread, axis=-1), both, preferred_element_type=f32)
        drawn = jnp.dot(jnp.concatenate(chosen, axis=-1), both, preferred_element_type=f32)
        if turn == 0:
            grad[...] = more
            pull[...] = drawn
        else:
            grad[...] += more
            pull[...] += drawn
    rest = jnp.sum(rest, axis=-1, keepdims=True)
    hit = jnp.sum(hits, axis=-1, keepdims=True)
    pooled = jnp.sum(pooled_target, axis=-1, keepdims=True)
    root = jnp.sqrt(sine_offset - pooled * pooled)
    margin = pooled * math.cos(margin_angle) - root * math.sin(margin_angle)
    own = hit * jnp.exp(logit_scale * margin)
    slope = hit * (math.cos(margin_angle) + pooled * math.sin(margin_angle) / root)
    unitf = unit.astype(f32)
    square = jnp.sum(unitf * unitf, axis=-1, keepdims=True) + 1e-30
    more = grad[...]
    more_along = jnp.sum(more * unitf, axis=-1, keepdims=True) / square
    sent[:, :width] = (more - more_along * unitf).astype(bf16)
    drawn = pull[...] * slope
    drawn_along = jnp.sum(drawn * unitf, axis=-1, keepdims=True) / square
    sent[:, width : 2 * width] = (drawn - drawn_along * unitf).astype(bf16)
    lanes = lax.broadcasted_iota(jnp.int32, (rows, 128), 1)
    packed = jnp.zeros((rows, 128), f32)
    for at, value in enumerate((rest, own, more_along, drawn_along)):
        high = value.astype(bf16).astype(f32)
        packed = jnp.where(lanes == 2 * at, high, packed)
        packed = jnp.where(lanes == 2 * at + 1, value - high, packed)
    sent[:, 2 * width :] = packed.astype(bf16)


def head_call(feature, centers, nsamp, nsub, nblk):
    rows, width = feature.shape[0], centers[0].shape[1]
    return pl.pallas_call(
        functools.partial(head_kernel, nsamp, nsub, nblk),
        out_shape=jax.ShapeDtypeStruct((rows, 2 * width + 128), bf16),
        in_specs=[VMEM] * (1 + len(centers)),
        out_specs=VMEM,
        scratch_shapes=[pltpu.VMEM((rows, width), f32), pltpu.VMEM((rows, width), f32)],
        name="head",
    )(feature, *centers)


def finish_kernel(parts, sent, direction, inverse, out):
    width = direction.shape[1]
    total = parts[0].astype(f32)
    for z in range(1, Z):
        total = total + parts[z].astype(f32)
    scalars = total[:, 2 * width :]
    rest, own, more_along, drawn_along = [
        lane_of(scalars, 2 * at) + lane_of(scalars, 2 * at + 1) for at in range(4)
    ]
    unitf = sent[0, :, :width].astype(f32)
    more = total[:, :width] + more_along * unitf
    drawn = total[:, width : 2 * width] + drawn_along * unitf
    whole = rest + own
    grad = logit_scale * (more / whole - (rest / whole) * drawn)
    unit = direction[...]
    along = jnp.sum(grad * unit, axis=-1, keepdims=True)
    out[...] = inverse[:, 0:1] * (grad - along * unit)


def finish_call(parts, sent, direction, inverse):
    return pl.pallas_call(
        finish_kernel,
        out_shape=jax.ShapeDtypeStruct(direction.shape, f32),
        in_specs=[VMEM] * 4,
        out_specs=VMEM,
        name="finish",
    )(parts, sent, direction, inverse)


def unit_rows(values):
    valf = values.astype(f32)
    inverse = lax.rsqrt(jnp.sum(valf * valf, axis=-1, keepdims=True) + 1e-06)
    return valf * inverse


def chain(rows, weight, gain, sections):
    index = lax.axis_index("section")
    first = (index == 0).astype(jnp.int32).reshape(1)
    count = rows.shape[0] // PIECES
    each = sections // PIECES
    home = [each * m + each - 1 for m in range(PIECES)]
    last = DELAY * (sections - 1)
    arrived, final = [], None
    for slot in range(PIECES + last):
        fresh = rows[slot * count : (slot + 1) * count] if slot < PIECES else None
        came = arrived[slot - DELAY] if slot >= DELAY else None
        done = section_call(first, fresh, came, weight, gain)
        route = [
            (s, s + 1) for s in range(sections - 1) if 0 <= slot - DELAY * s < PIECES
        ]
        piece = slot - last
        if piece >= 0 and home[piece] != sections - 1:
            route.append((sections - 1, home[piece]))
        if route:
            arrived.append(lax.ppermute(done, "section", route))
        if piece >= 0:
            if home[piece] == sections - 1:
                final = jnp.where(index == sections - 1, done, final)
            elif final is None:
                final = arrived[-1]
            else:
                final = jnp.where(index == home[piece], arrived[-1], final)
    part = count // each
    while part < final.shape[0]:
        half = final.shape[0] // 2
        gap = half // part
        route = [(p, p - gap) for p in range(2 * gap - 1, sections, 2 * gap)]
        other = lax.ppermute(final[:half], "section", route)
        kept = index % (2 * gap) == 2 * gap - 1
        final = jnp.where(kept, final[half:], other)
    return final


def shards(inputs, section_weight, section_gain, neck_weight, centers, sampled, labels):
    sections = lax.axis_size("section")
    shard_index = lax.axis_index("ident")
    _, nsamp, nsub, nblk, width = centers.shape
    unit_centers = unit_rows(centers[0].reshape(-1, width)).astype(bf16)
    tags = jnp.concatenate([shard_index.reshape(1), sampled[0]]).astype(f32)
    tags = jnp.concatenate([tags, jnp.zeros((16 - 1 - nsamp,), f32)])
    tail = jnp.broadcast_to(tags[:, None], (16, width)).astype(bf16)
    mine = jnp.concatenate([unit_centers, tail], axis=0)
    line = [mine] + [lax.ppermute(mine, "ident", ident_route(dx=d)) for d in (1, 3, 2)]
    line += [lax.ppermute(block, "ident", ident_route(flip=1)) for block in line]
    code = labels[0][:, None]
    lanes = jnp.arange(128, dtype=jnp.int32)[None, :]
    digits = jnp.where(
        lanes == 0,
        code // (BLOCKS_DEV * nblk),
        jnp.where(lanes == 1, code // nblk % BLOCKS_DEV, jnp.where(lanes == 2, code % nblk, 0)),
    ).astype(bf16)
    own = chain(inputs[0], section_weight[0], section_gain, sections)
    sent, direction, inverse = neck_call(own, neck_weight, digits)
    gathered = lax.all_to_all(sent, "ident", 0, 0, axis_index_groups=Z_GROUPS, tiled=True)
    partial = head_call(gathered.reshape(-1, gathered.shape[-1]), line, nsamp, nsub, nblk)
    parts = lax.all_to_all(
        partial.reshape(Z, -1, partial.shape[-1]), "ident", 0, 0, axis_index_groups=Z_GROUPS, tiled=True
    )
    return finish_call(parts, sent, direction, inverse)[None]


def solution(mesh):
    in_specs = (
        P("ident", None, None),
        P("section", None, None),
        P("section", None),
        P(),
        P("ident", None, None, None, None),
        P("ident", None),
        P("ident", "section"),
    )
    out_specs = P("ident", "section", None)
    return jax.shard_map(shards, mesh=mesh, in_specs=in_specs, out_specs=out_specs, check_vma=False)
```
